32 devices in a mesh: gx: 2 (over x), yz: 16 (over z, y, core).
Axes of the slice: x: 2, y: 2, z: 4, core: 2. Of those that a mesh axis runs over, the one named last changes fastest.
Arguments:
- tensor: float32 [4, 512, 32, 32], P(None, 'gx', 'yz'), may hold values from -40 to 40
- start_basis: float32 [96, 512], replicated, may hold values from -6 to 6
Outputs:
- core_tensor: float32 [32, 32, 384], P(('gx', 'yz'))
- factor: float32 [96, 512], replicated
The draws below stay inside these ranges and needn't reach their ends.
All inputs are finite; a program needn't handle non-finite values.
Results may differ from the reference program's by a relative error of at most 0.00012.
Values sent between devices are 32-bit elements; how exact they have to be, the bound alone decides.
A program may use at most 64 MiB of HBM per device.

```python
import math
import jax
import jax.numpy as jnp
from jax import lax

S = 4
NX = 512
K = 96
NY = 32
NZ = 32


def draw_tensor(key, part):
    keys_all = jax.random.split(jax.random.fold_in(key, 17), 5)
    full_shape = (S, NX, NY, NZ)
    row_scale = 0.2 * jnp.exp(jax.random.uniform(keys_all[0], (NX,), jnp.float32, 0.0, math.log(2.5)))
    line_scale = 0.3 * jnp.exp(jax.random.uniform(keys_all[1], (NY,), jnp.float32, 0.0, math.log(10.0)))
    noise = jnp.clip(jax.random.normal(keys_all[2], full_shape, jnp.float32), -5.0, 5.0)
    components = 4
    load_rows = jax.random.uniform(keys_all[3], (components, NX), jnp.float32, -0.15, 0.15)
    factors = jnp.clip(jax.random.normal(keys_all[4], (components, S, NY, NZ), jnp.float32), -4.0, 4.0)
    shared = jnp.zeros(full_shape, jnp.float32)
    for component in range(components):
        shared = shared + load_rows[component][None, :, None, None] * factors[component][:, None, :, :]
    return row_scale[None, :, None, None] * line_scale[None, None, :, None] * (noise + shared)


def bell_draw(stream_key, extent, spread, limit, held_as=jnp.bfloat16):
    return jnp.clip(spread * jax.random.normal(stream_key, extent, jnp.float32), -limit, limit).astype(held_as)


def setup_inputs(seed: int = 0) -> dict:
    streams_of = jax.random.split(jax.random.key(seed), 3)
    return {
        "tensor": draw_tensor(jax.random.fold_in(streams_of[2], 71), 0),
        "start_basis": bell_draw(streams_of[1], (K, NX), 1.0, 6.0, jnp.float32),
    }


def orthonormal(image_rows):
    small_gram = jnp.dot(image_rows, image_rows.T, precision=lax.Precision.HIGHEST)
    lower_factor = jnp.linalg.cholesky(small_gram)
    return lax.linalg.triangular_solve(lower_factor, image_rows, left_side=True, lower=True)

def reference(tensor, start_basis):
    cell_count = S * NY * NZ

    def accumulate(line_index, gram_matrix):
        plane = lax.dynamic_slice_in_dim(tensor, line_index, 1, 2)
        return gram_matrix + lax.dot_general(plane, plane, (((0, 2, 3), (0, 2, 3)), ((), ())), precision=lax.Precision.HIGHEST)
    gram_matrix = lax.fori_loop(0, NY, accumulate, jnp.zeros((NX, NX), jnp.float32)) / cell_count
    basis = start_basis
    for repeat in range(2):
        basis = orthonormal(jnp.dot(basis, gram_matrix, precision=lax.Precision.HIGHEST))
    core_tensor = jnp.einsum('kx,sxyz->zysk', basis, tensor, precision=lax.Precision.HIGHEST)
    return (core_tensor.reshape(NZ, NY, S * K), basis)
```

```python
import functools

import jax
import jax.numpy as jnp
from jax import lax
from jax.experimental import pallas as pl
from jax.experimental.pallas import tpu as pltpu
from jax.sharding import PartitionSpec as P

HIGHEST = lax.Precision.HIGHEST
LANES = 128
SUBLANES = 8


def mm(a, b):
    return lax.dot_general(
        a, b, (((1,), (0,)), ((), ())), precision=HIGHEST, preferred_element_type=jnp.float32
    )


def mm_nt(a, b):
    return lax.dot_general(
        a, b, (((1,), (1,)), ((), ())), precision=HIGHEST, preferred_element_type=jnp.float32
    )


def inverse_cholesky(gram):
    rank = gram.shape[0]
    wide = -(-rank // LANES) * LANES
    row_id = lax.broadcasted_iota(jnp.int32, (rank, wide), 0)
    lane_id = lax.broadcasted_iota(jnp.int32, (rank, wide), 1)
    left = jnp.concatenate([gram, jnp.zeros((rank, wide - rank), jnp.float32)], axis=1) if wide > rank else gram
    right = jnp.where(row_id == lane_id, 1.0, 0.0).astype(jnp.float32)
    done_left, done_right = [], []
    for base in range(0, rank, SUBLANES):
        rows = rank - base
        local_row = lax.broadcasted_iota(jnp.int32, (rows, wide), 0)
        for step in range(SUBLANES):
            column = base + step
            pivot = left[step : step + 1, column : column + 1]
            inverse = 1.0 / jnp.broadcast_to(pivot, (1, wide))
            row_left = left[step : step + 1, :] * inverse
            row_right = right[step : step + 1, :] * inverse
            factor = jnp.broadcast_to(left[:, column : column + 1], (rows, wide))
            factor = jnp.where(local_row > step, factor, 0.0)
            left = left - factor * row_left
            right = right - factor * row_right
        done_left.append(left[:SUBLANES])
        done_right.append(right[:SUBLANES])
        left, right = left[SUBLANES:], right[SUBLANES:]
    upper = jnp.concatenate(done_left, axis=0)
    lower = jnp.concatenate(done_right, axis=0)
    pivots = jnp.sum(jnp.where(row_id == lane_id, upper, 0.0), axis=1, keepdims=True)
    return (lower / jnp.sqrt(pivots))[:, :rank]


def kernel(
    shape,
    x_ref,
    start_ref,
    core_ref,
    factor_ref,
    xg,
    stage,
    sums,
    parts,
    core_out,
    core_in,
    x_send,
    x_recv,
    send_sem,
    recv_sem,
):
    n_gx, n_yz, cell_count, rows = shape
    n = n_gx * n_yz
    my_x, my_yz = lax.axis_index("gx"), lax.axis_index("yz")
    me = my_x * n_yz + my_yz
    species, _, cells_z, width = x_ref.shape
    lines = xg.shape[2]
    rank, total = start_ref.shape
    per_column = rank // rows

    def place(flat):
        return {"gx": lax.div(flat, n_yz), "yz": lax.rem(flat, n_yz)}

    def ahead(k):
        return lax.rem(me + k, n)

    def behind(k):
        return lax.rem(me + n - k, n)

    barrier = pltpu.get_barrier_semaphore()

    @pl.loop(1, n)
    def _(k):
        pl.semaphore_signal(barrier, inc=1, device_id=place(ahead(k)), device_id_type=pl.DeviceIdType.MESH)

    xg[my_x] = x_ref[:, pl.ds(my_x * lines, lines)]
    pl.semaphore_wait(barrier, n - 1)

    def x_copy(k):
        peer = lax.rem(my_x + k, n_gx)
        return pltpu.make_async_remote_copy(
            src_ref=x_ref.at[:, pl.ds(peer * lines, lines)],
            dst_ref=xg.at[my_x],
            send_sem=x_send.at[k - 1],
            recv_sem=x_recv.at[k - 1],
            device_id={"gx": peer, "yz": my_yz},
            device_id_type=pl.DeviceIdType.MESH,
        )

    for k in range(1, n_gx):
        x_copy(k).start()
    for k in range(1, n_gx):
        x_copy(k).wait()

    def held(part):
        return xg[part].reshape(species * lines * cells_z, width)

    def image_of(basis):
        projected = None
        for part in range(n_gx):
            term = mm_nt(basis[:, part * width : (part + 1) * width], held(part))
            projected = term if projected is None else projected + term
        projected = projected * (1.0 / cell_count)
        return jnp.concatenate([mm(projected, held(part)) for part in range(n_gx)], axis=1)

    def scatter_copy(turn, k):
        peer = ahead(k)
        return pltpu.make_async_remote_copy(
            src_ref=stage.at[turn, peer],
            dst_ref=parts.at[turn, k - 1],
            send_sem=send_sem.at[k - 1],
            recv_sem=recv_sem.at[2 * turn, k - 1],
            device_id=place(peer),
            device_id_type=pl.DeviceIdType.MESH,
        )

    def gather_copy(turn, k):
        return pltpu.make_async_remote_copy(
            src_ref=sums.at[turn, me],
            dst_ref=sums.at[turn, me],
            send_sem=send_sem.at[k - 1],
            recv_sem=recv_sem.at[2 * turn + 1, k - 1],
            device_id=place(ahead(k)),
            device_id_type=pl.DeviceIdType.MESH,
        )

    def gather_arrival(turn, k):
        source = behind(k)
        return pltpu.make_async_remote_copy(
            src_ref=sums.at[turn, me],
            dst_ref=sums.at[turn, source],
            send_sem=send_sem.at[k - 1],
            recv_sem=recv_sem.at[2 * turn + 1, k - 1],
            device_id=place(ahead(k)),
            device_id_type=pl.DeviceIdType.MESH,
        )

    def start_scatter(turn, image):
        for owner in range(n):
            column, block = owner // per_column, owner % per_column
            stage[turn, owner] = image[block * rows : (block + 1) * rows, column * LANES : (column + 1) * LANES]

        @pl.loop(1, n)
        def _(k):
            scatter_copy(turn, k).start()

    def finish_sum(turn):
        @pl.loop(1, n)
        def _(k):
            scatter_copy(turn, k).wait()

        terms = [stage[turn, me]] + [parts[turn, k] for k in range(n - 1)]
        while len(terms) > 1:
            terms = [a + b for a, b in zip(terms[::2], terms[1::2])] + ([terms[-1]] if len(terms) % 2 else [])
        sums[turn, me] = terms[0]

        @pl.loop(1, n)
        def _(k):
            gather_copy(turn, k).start()

        @pl.loop(1, n)
        def _(k):
            gather_arrival(turn, k).wait()

        columns = []
        for column in range(total // LANES):
            blocks = [sums[turn, column * per_column + block] for block in range(per_column)]
            columns.append(jnp.concatenate(blocks, axis=0))
        return jnp.concatenate(columns, axis=1)

    start_scatter(0, image_of(start_ref[...]))
    image = finish_sum(0)
    start_scatter(1, image_of(image))
    inverse = inverse_cholesky(mm_nt(image, image))
    image = mm(inverse, finish_sum(1))
    basis = mm(inverse_cholesky(mm_nt(image, image)), image)
    factor_ref[...] = basis

    truncated = None
    for part in range(n_gx):
        term = mm_nt(held(part), basis[:, part * width : (part + 1) * width])
        truncated = term if truncated is None else truncated + term
    share = cells_z // n
    for s in range(species):
        for line in range(lines):
            at = (s * lines + line) * cells_z
            core_out[:, line, s * rank : (s + 1) * rank] = truncated[at : at + cells_z]

    mine = my_yz * n_gx + my_x

    def core_copy(k):
        peer = ahead(k)
        return pltpu.make_async_remote_copy(
            src_ref=core_out.at[pl.ds(peer * share, share)],
            dst_ref=core_in.at[mine],
            send_sem=send_sem.at[k - 1],
            recv_sem=recv_sem.at[4, k - 1],
            device_id=place(peer),
            device_id_type=pl.DeviceIdType.MESH,
        )

    def core_arrival(k):
        source = behind(k)
        place_of = lax.rem(source, n_yz) * n_gx + lax.div(source, n_yz)
        return pltpu.make_async_remote_copy(
            src_ref=core_out.at[pl.ds(ahead(k) * share, share)],
            dst_ref=core_in.at[place_of],
            send_sem=send_sem.at[k - 1],
            recv_sem=recv_sem.at[4, k - 1],
            device_id=place(ahead(k)),
            device_id_type=pl.DeviceIdType.MESH,
        )

    @pl.loop(1, n)
    def _(k):
        core_copy(k).start()

    core_in[mine] = core_out[pl.ds(me * share, share)]

    @pl.loop(1, n)
    def _(k):
        core_arrival(k).wait()

    core_ref[...] = core_in[...]


def kernel_program(tensor, start_basis, n_gx, n_yz, rows):
    n = n_gx * n_yz
    species, width, lines_held, cells_z = tensor.shape
    rank, total = start_basis.shape
    lines = lines_held // n_gx
    cell_count = species * lines_held * n_yz * cells_z
    share = cells_z // n
    out = species * rank
    core, factor = pl.pallas_call(
        functools.partial(kernel, (n_gx, n_yz, cell_count, rows)),
        out_shape=(
            jax.ShapeDtypeStruct((n, share, lines, out), jnp.float32),
            jax.ShapeDtypeStruct((rank, total), jnp.float32),
        ),
        in_specs=[pl.BlockSpec(memory_space=pltpu.VMEM)] * 2,
        out_specs=(pl.BlockSpec(memory_space=pltpu.VMEM),) * 2,
        scratch_shapes=[
            pltpu.VMEM((n_gx, species, lines, cells_z, width), jnp.float32),
            pltpu.VMEM((2, n, rows, LANES), jnp.float32),
            pltpu.VMEM((2, n, rows, LANES), jnp.float32),
            pltpu.VMEM((2, n - 1, rows, LANES), jnp.float32),
            pltpu.VMEM((cells_z, lines, out), jnp.float32),
            pltpu.VMEM((n, share, lines, out), jnp.float32),
            pltpu.SemaphoreType.DMA((n_gx - 1,)),
            pltpu.SemaphoreType.DMA((n_gx - 1,)),
            pltpu.SemaphoreType.DMA((n - 1,)),
            pltpu.SemaphoreType.DMA((5, n - 1)),
        ],
        compiler_params=pltpu.CompilerParams(collective_id=0, has_side_effects=True),
    )(tensor.transpose(0, 2, 3, 1), start_basis)
    core = core.transpose(1, 0, 2, 3).reshape(share, n * lines, out)
    return core, factor


def orthonormal(image_rows):
    small_gram = jnp.dot(image_rows, image_rows.T, precision=HIGHEST)
    lower_factor = jnp.linalg.cholesky(small_gram)
    return lax.linalg.triangular_solve(lower_factor, image_rows, left_side=True, lower=True)


def collective_program(tensor, start_basis):
    regrouped = lax.all_to_all(tensor, "gx", split_axis=2, concat_axis=1, tiled=True)
    species, _, lines, cells_z = regrouped.shape
    cell_count = species * lines * lax.axis_size("gx") * lax.axis_size("yz") * cells_z
    gram_matrix = lax.dot_general(
        regrouped, regrouped, (((0, 2, 3), (0, 2, 3)), ((), ())), precision=HIGHEST
    )
    gram_matrix = lax.psum(gram_matrix, ("gx", "yz")) / cell_count
    basis = start_basis
    for _ in range(2):
        basis = orthonormal(jnp.dot(basis, gram_matrix, precision=HIGHEST))
    core_local = jnp.einsum("kx,sxyz->zysk", basis, regrouped, precision=HIGHEST)
    core_local = core_local.reshape(cells_z, lines, species * basis.shape[0])
    core_tensor = lax.all_to_all(
        lax.all_to_all(core_local, "gx", split_axis=0, concat_axis=1, tiled=True),
        "yz",
        split_axis=0,
        concat_axis=1,
        tiled=True,
    )
    return core_tensor, basis


def solution(mesh):
    n_gx, n_yz = mesh.shape["gx"], mesh.shape["yz"]
    n = n_gx * n_yz

    def local(tensor, start_basis):
        rank, total = start_basis.shape
        rows, left_over = divmod(rank * (total // LANES), n)
        whole_rows = left_over == 0 and total % LANES == 0 and rank % max(rows, 1) == 0 and rank % SUBLANES == 0
        if whole_rows and tensor.shape[1] % LANES == 0:
            return kernel_program(tensor, start_basis, n_gx, n_yz, rows)
        return collective_program(tensor, start_basis)

    return jax.shard_map(
        local,
        mesh=mesh,
        in_specs=(P(None, "gx", "yz", None), P()),
        out_specs=(P(("gx", "yz"), None, None), P()),
        check_vma=False,
    )
```

```python
import functools

import jax
import jax.numpy as jnp
from jax import lax
from jax.experimental import pallas as pl
from jax.experimental.pallas import tpu as pltpu
from jax.sharding import PartitionSpec as P

HIGHEST = lax.Precision.HIGHEST
LANES = 128
SUBLANES = 8


def mm(a, b):
    return lax.dot_general(
        a, b, (((1,), (0,)), ((), ())), precision=HIGHEST, preferred_element_type=jnp.float32
    )


def mm_nt(a, b):
    return lax.dot_general(
        a, b, (((1,), (1,)), ((), ())), precision=HIGHEST, preferred_element_type=jnp.float32
    )


def inverse_cholesky(gram, panel=SUBLANES):
    rank = gram.shape[0]
    wide = -(-rank // LANES) * LANES
    row_id = lax.broadcasted_iota(jnp.int32, (rank, wide), 0)
    lane_id = lax.broadcasted_iota(jnp.int32, (rank, wide), 1)
    left = jnp.concatenate([gram, jnp.zeros((rank, wide - rank), jnp.float32)], axis=1) if wide > rank else gram
    right = jnp.where(row_id == lane_id, 1.0, 0.0).astype(jnp.float32)
    done_right, done_pivots = [], []
    for base in range(0, rank, SUBLANES):
        rows = rank - base
        local_row = lax.broadcasted_iota(jnp.int32, (rows, wide), 0)
        pivots = jnp.zeros((SUBLANES, wide), jnp.float32)
        for first in range(0, SUBLANES, panel):
            spread = [
                jnp.broadcast_to(left[:, base + step : base + step + 1], (rows, wide))
                for step in range(first, first + panel)
            ]
            for step in range(first, first + panel):
                column = spread[step - first]
                pivot = column[step : step + 1]
                pivots = jnp.where(local_row[:SUBLANES] == step, jnp.broadcast_to(pivot, (SUBLANES, wide)), pivots)
                factor = jnp.where(local_row > step, column * (1.0 / pivot), 0.0)
                for other in range(step + 1, first + panel):
                    spread[other - first] = spread[other - first] - factor * spread[other - first][step : step + 1]
                left = left - factor * left[step : step + 1]
                right = right - factor * right[step : step + 1]
        done_right.append(right[:SUBLANES] / jnp.sqrt(pivots))
        left, right = left[SUBLANES:], right[SUBLANES:]
    return jnp.concatenate(done_right, axis=0)[:, :rank]


def kernel(
    shape,
    x_ref,
    start_ref,
    core_ref,
    factor_ref,
    xg,
    stage,
    sums,
    parts,
    core_out,
    core_in,
    x_send,
    x_recv,
    send_sem,
    recv_sem,
):
    n_gx, n_yz, cell_count, rows = shape
    n = n_gx * n_yz
    my_x, my_yz = lax.axis_index("gx"), lax.axis_index("yz")
    me = my_x * n_yz + my_yz
    species, _, cells_z, width = x_ref.shape
    lines = xg.shape[2]
    rank, total = start_ref.shape
    per_column = rank // rows
    order = range(n - 1, 0, -1)
    flips = [1 - 2 * lax.rem(lax.div(me, 1 << bit), 2) for bit in range(n.bit_length() - 1)]

    def place(flat):
        return {"gx": lax.div(flat, n_yz), "yz": lax.rem(flat, n_yz)}

    def partner(k):
        return me + sum((1 << bit) * flip for bit, flip in enumerate(flips) if k >> bit & 1)

    barrier = pltpu.get_barrier_semaphore()

    for k in order:
        pl.semaphore_signal(barrier, inc=1, device_id=place(partner(k)), device_id_type=pl.DeviceIdType.MESH)

    xg[my_x] = x_ref[:, pl.ds(my_x * lines, lines)]
    pl.semaphore_wait(barrier, n - 1)

    def x_copy(k):
        peer = lax.rem(my_x + k, n_gx)
        return pltpu.make_async_remote_copy(
            src_ref=x_ref.at[:, pl.ds(peer * lines, lines)],
            dst_ref=xg.at[my_x],
            send_sem=x_send.at[k - 1],
            recv_sem=x_recv.at[k - 1],
            device_id={"gx": peer, "yz": my_yz},
            device_id_type=pl.DeviceIdType.MESH,
        )

    for k in range(1, n_gx):
        x_copy(k).start()
    for k in range(1, n_gx):
        x_copy(k).wait()

    def held(part):
        return xg[part].reshape(species * lines * cells_z, width)

    def image_of(basis):
        projected = None
        for part in range(n_gx):
            term = mm_nt(basis[:, part * width : (part + 1) * width], held(part))
            projected = term if projected is None else projected + term
        projected = projected * (1.0 / cell_count)
        return jnp.concatenate([mm(projected, held(part)) for part in range(n_gx)], axis=1)

    def scatter_copy(turn, k):
        peer = partner(k)
        return pltpu.make_async_remote_copy(
            src_ref=stage.at[turn, peer],
            dst_ref=parts.at[turn, k - 1],
            send_sem=send_sem.at[2 * turn, k - 1],
            recv_sem=recv_sem.at[2 * turn, k - 1],
            device_id=place(peer),
            device_id_type=pl.DeviceIdType.MESH,
        )

    def gather_copy(turn, k):
        return pltpu.make_async_remote_copy(
            src_ref=sums.at[turn, me],
            dst_ref=sums.at[turn, me],
            send_sem=send_sem.at[2 * turn + 1, k - 1],
            recv_sem=recv_sem.at[2 * turn + 1, k - 1],
            device_id=place(partner(k)),
            device_id_type=pl.DeviceIdType.MESH,
        )

    def gather_arrival(turn, k):
        source = partner(k)
        return pltpu.make_async_remote_copy(
            src_ref=sums.at[turn, me],
            dst_ref=sums.at[turn, source],
            send_sem=send_sem.at[2 * turn + 1, k - 1],
            recv_sem=recv_sem.at[2 * turn + 1, k - 1],
            device_id=place(partner(k)),
            device_id_type=pl.DeviceIdType.MESH,
        )

    def start_scatter(turn, image):
        for owner in range(n):
            column, block = owner // per_column, owner % per_column
            stage[turn, owner] = image[block * rows : (block + 1) * rows, column * LANES : (column + 1) * LANES]
        for k in order:
            scatter_copy(turn, k).start()

    def start_gather(turn):
        for k in order:
            scatter_copy(turn, k).wait_recv()
        terms = [stage[turn, me]] + [parts[turn, k] for k in range(n - 1)]
        while len(terms) > 1:
            terms = [a + b for a, b in zip(terms[::2], terms[1::2])] + ([terms[-1]] if len(terms) % 2 else [])
        sums[turn, me] = terms[0]
        for k in order:
            gather_copy(turn, k).start()
        for k in order:
            scatter_copy(turn, k).wait_send()

    def gathered(turn):
        for k in order:
            gather_arrival(turn, k).wait_recv()
        blocks = [sums[turn, owner] for owner in range(n)]
        columns = [jnp.concatenate(blocks[at : at + per_column], axis=0) for at in range(0, n, per_column)]
        return jnp.concatenate(columns, axis=1)

    start_scatter(0, image_of(start_ref[...]))
    start_gather(0)
    image = gathered(0)
    start_scatter(1, image_of(image))
    start_gather(1)
    inverse = inverse_cholesky(mm_nt(image, image))
    image = mm(inverse, gathered(1))
    basis = mm(inverse_cholesky(mm_nt(image, image)), image)
    factor_ref[...] = basis

    truncated = None
    for part in range(n_gx):
        term = mm_nt(held(part), basis[:, part * width : (part + 1) * width])
        truncated = term if truncated is None else truncated + term
    share = cells_z // n
    for s in range(species):
        for line in range(lines):
            at = (s * lines + line) * cells_z
            core_out[:, line, s * rank : (s + 1) * rank] = truncated[at : at + cells_z]

    mine = my_yz * n_gx + my_x

    def core_copy(k):
        peer = partner(k)
        return pltpu.make_async_remote_copy(
            src_ref=core_out.at[pl.ds(peer * share, share)],
            dst_ref=core_in.at[mine],
            send_sem=send_sem.at[4, k - 1],
            recv_sem=recv_sem.at[4, k - 1],
            device_id=place(peer),
            device_id_type=pl.DeviceIdType.MESH,
        )

    def core_arrival(k):
        source = partner(k)
        place_of = lax.rem(source, n_yz) * n_gx + lax.div(source, n_yz)
        return pltpu.make_async_remote_copy(
            src_ref=core_out.at[pl.ds(partner(k) * share, share)],
            dst_ref=core_in.at[place_of],
            send_sem=send_sem.at[4, k - 1],
            recv_sem=recv_sem.at[4, k - 1],
            device_id=place(partner(k)),
            device_id_type=pl.DeviceIdType.MESH,
        )

    for k in order:
        core_copy(k).start()

    core_in[mine] = core_out[pl.ds(me * share, share)]

    for k in order:
        for turn in range(2):
            gather_copy(turn, k).wait_send()
        core_arrival(k).wait()

    core_ref[...] = core_in[...]


def kernel_program(tensor, start_basis, n_gx, n_yz, rows):
    n = n_gx * n_yz
    species, width, lines_held, cells_z = tensor.shape
    rank, total = start_basis.shape
    lines = lines_held // n_gx
    cell_count = species * lines_held * n_yz * cells_z
    share = cells_z // n
    out = species * rank
    core, factor = pl.pallas_call(
        functools.partial(kernel, (n_gx, n_yz, cell_count, rows)),
        out_shape=(
            pltpu.VMEM((n, share, lines, out), jnp.float32),
            pltpu.VMEM((rank, total), jnp.float32),
        ),
        in_specs=[pl.BlockSpec(memory_space=pltpu.VMEM)] * 2,
        out_specs=(pl.BlockSpec(memory_space=pltpu.VMEM),) * 2,
        scratch_shapes=[
            pltpu.VMEM((n_gx, species, lines, cells_z, width), jnp.float32),
            pltpu.VMEM((2, n, rows, LANES), jnp.float32),
            pltpu.VMEM((2, n, rows, LANES), jnp.float32),
            pltpu.VMEM((2, n - 1, rows, LANES), jnp.float32),
            pltpu.VMEM((cells_z, lines, out), jnp.float32),
            pltpu.VMEM((n, share, lines, out), jnp.float32),
            pltpu.SemaphoreType.DMA((n_gx - 1,)),
            pltpu.SemaphoreType.DMA((n_gx - 1,)),
            pltpu.SemaphoreType.DMA((5, n - 1)),
            pltpu.SemaphoreType.DMA((5, n - 1)),
        ],
        compiler_params=pltpu.CompilerParams(collective_id=0, has_side_effects=True),
    )(tensor.transpose(0, 2, 3, 1), start_basis)
    core = core.transpose(1, 0, 2, 3).reshape(share, n * lines, out)
    return core, factor


def orthonormal(image_rows):
    small_gram = jnp.dot(image_rows, image_rows.T, precision=HIGHEST)
    lower_factor = jnp.linalg.cholesky(small_gram)
    return lax.linalg.triangular_solve(lower_factor, image_rows, left_side=True, lower=True)


def collective_program(tensor, start_basis):
    regrouped = lax.all_to_all(tensor, "gx", split_axis=2, concat_axis=1, tiled=True)
    species, _, lines, cells_z = regrouped.shape
    cell_count = species * lines * lax.axis_size("gx") * lax.axis_size("yz") * cells_z
    gram_matrix = lax.dot_general(
        regrouped, regrouped, (((0, 2, 3), (0, 2, 3)), ((), ())), precision=HIGHEST
    )
    gram_matrix = lax.psum(gram_matrix, ("gx", "yz")) / cell_count
    basis = start_basis
    for _ in range(2):
        basis = orthonormal(jnp.dot(basis, gram_matrix, precision=HIGHEST))
    core_local = jnp.einsum("kx,sxyz->zysk", basis, regrouped, precision=HIGHEST)
    core_local = core_local.reshape(cells_z, lines, species * basis.shape[0])
    core_tensor = lax.all_to_all(
        lax.all_to_all(core_local, "gx", split_axis=0, concat_axis=1, tiled=True),
        "yz",
        split_axis=0,
        concat_axis=1,
        tiled=True,
    )
    return core_tensor, basis


def solution(mesh):
    n_gx, n_yz = mesh.shape["gx"], mesh.shape["yz"]
    n = n_gx * n_yz

    def local(tensor, start_basis):
        rank, total = start_basis.shape
        rows, left_over = divmod(rank * (total // LANES), n)
        whole_rows = left_over == 0 and total % LANES == 0 and n & (n - 1) == 0
        whole_rows = whole_rows and rank % max(rows, 1) == 0 and rank % SUBLANES == 0
        if whole_rows and tensor.shape[1] % LANES == 0:
            return kernel_program(tensor, start_basis, n_gx, n_yz, rows)
        return collective_program(tensor, start_basis)

    return jax.shard_map(
        local,
        mesh=mesh,
        in_specs=(P(None, "gx", "yz", None), P()),
        out_specs=(P(("gx", "yz"), None, None), P()),
        check_vma=False,
    )
```

```python
import functools

import jax
import jax.numpy as jnp
from jax import lax
from jax.experimental import pallas as pl
from jax.experimental.pallas import tpu as pltpu
from jax.sharding import PartitionSpec as P

HIGHEST = lax.Precision.HIGHEST
LANES = 128
SUBLANES = 8


def mm(a, b):
    return lax.dot_general(
        a, b, (((1,), (0,)), ((), ())), precision=HIGHEST, preferred_element_type=jnp.float32
    )


def mm_nt(a, b):
    return lax.dot_general(
        a, b, (((1,), (1,)), ((), ())), precision=HIGHEST, preferred_element_type=jnp.float32
    )


def inverse_cholesky(gram, panel=SUBLANES):
    rank = gram.shape[0]
    wide = -(-rank // LANES) * LANES
    row_id = lax.broadcasted_iota(jnp.int32, (rank, wide), 0)
    lane_id = lax.broadcasted_iota(jnp.int32, (rank, wide), 1)
    left = jnp.concatenate([gram, jnp.zeros((rank, wide - rank), jnp.float32)], axis=1) if wide > rank else gram
    right = jnp.where(row_id == lane_id, 1.0, 0.0).astype(jnp.float32)
    done_right, done_pivots = [], []
    for base in range(0, rank, SUBLANES):
        rows = rank - base
        local_row = lax.broadcasted_iota(jnp.int32, (rows, wide), 0)
        pivots = jnp.zeros((SUBLANES, wide), jnp.float32)
        for first in range(0, SUBLANES, panel):
            spread = [
                jnp.broadcast_to(left[:, base + step : base + step + 1], (rows, wide))
                for step in range(first, first + panel)
            ]
            for step in range(first, first + panel):
                column = spread[step - first]
                pivot = column[step : step + 1]
                pivots = jnp.where(local_row[:SUBLANES] == step, jnp.broadcast_to(pivot, (SUBLANES, wide)), pivots)
                factor = jnp.where(local_row > step, column * (1.0 / pivot), 0.0)
                for other in range(step + 1, first + panel):
                    spread[other - first] = spread[other - first] - factor * spread[other - first][step : step + 1]
                left = left - factor * left[step : step + 1]
                right = right - factor * right[step : step + 1]
        done_right.append(right[:SUBLANES] / jnp.sqrt(pivots))
        left, right = left[SUBLANES:], right[SUBLANES:]
    return jnp.concatenate(done_right, axis=0)[:, :rank]


def kernel(
    shape,
    x_ref,
    start_ref,
    core_ref,
    factor_ref,
    xg,
    stage,
    sums,
    pairs,
    parts,
    core_out,
    core_in,
    x_send,
    x_recv,
    send_sem,
    recv_sem,
):
    n_gx, n_yz, cell_count, rows = shape
    n = n_gx * n_yz
    my_x, my_yz = lax.axis_index("gx"), lax.axis_index("yz")
    me = my_x * n_yz + my_yz
    species, _, cells_z, width = x_ref.shape
    lines = xg.shape[2]
    rank, total = start_ref.shape
    per_column = rank // rows
    order = range(n - 1, 0, -1)
    odds = range(n - 1, 0, -2)
    direct = [*range(n - 2, 0, -2), 1]
    flips = [1 - 2 * lax.rem(lax.div(me, 1 << bit), 2) for bit in range(n.bit_length() - 1)]

    def place(flat):
        return {"gx": lax.div(flat, n_yz), "yz": lax.rem(flat, n_yz)}

    def partner(k):
        return me + sum((1 << bit) * flip for bit, flip in enumerate(flips) if k >> bit & 1)

    barrier = pltpu.get_barrier_semaphore()

    for k in order:
        pl.semaphore_signal(barrier, inc=1, device_id=place(partner(k)), device_id_type=pl.DeviceIdType.MESH)

    xg[my_x] = x_ref[:, pl.ds(my_x * lines, lines)]
    pl.semaphore_wait(barrier, n - 1)

    def x_copy(k):
        peer = lax.rem(my_x + k, n_gx)
        return pltpu.make_async_remote_copy(
            src_ref=x_ref.at[:, pl.ds(peer * lines, lines)],
            dst_ref=xg.at[my_x],
            send_sem=x_send.at[k - 1],
            recv_sem=x_recv.at[k - 1],
            device_id={"gx": peer, "yz": my_yz},
            device_id_type=pl.DeviceIdType.MESH,
        )

    for k in range(1, n_gx):
        x_copy(k).start()
    for k in range(1, n_gx):
        x_copy(k).wait()

    def held(part):
        return xg[part].reshape(species * lines * cells_z, width)

    def image_of(basis):
        projected = None
        for part in range(n_gx):
            term = mm_nt(basis[:, part * width : (part + 1) * width], held(part))
            projected = term if projected is None else projected + term
        projected = projected * (1.0 / cell_count)
        return jnp.concatenate([mm(projected, held(part)) for part in range(n_gx)], axis=1)

    def scatter_copy(turn, k):
        odd = k % 2
        return pltpu.make_async_remote_copy(
            src_ref=stage.at[turn, partner(k)],
            dst_ref=pairs.at[turn, k // 2] if odd else parts.at[turn, k // 2 - 1],
            send_sem=send_sem.at[2 * turn, k - 1],
            recv_sem=recv_sem.at[2 * turn, k - 1],
            device_id=place(partner(1) if odd else partner(k)),
            device_id_type=pl.DeviceIdType.MESH,
        )

    def gather_copy(turn, k):
        return pltpu.make_async_remote_copy(
            src_ref=sums.at[turn, me],
            dst_ref=sums.at[turn, me],
            send_sem=send_sem.at[2 * turn + 1, k - 1],
            recv_sem=recv_sem.at[2 * turn + 1, k - 1],
            device_id=place(partner(k)),
            device_id_type=pl.DeviceIdType.MESH,
        )

    def relay_copy(turn, k):
        source = partner(k)
        return pltpu.make_async_remote_copy(
            src_ref=sums.at[turn, source],
            dst_ref=sums.at[turn, source],
            send_sem=send_sem.at[2 * turn + 1, k],
            recv_sem=recv_sem.at[2 * turn + 1, k],
            device_id=place(partner(1)),
            device_id_type=pl.DeviceIdType.MESH,
        )

    def gather_arrival(turn, k):
        source = partner(k)
        return pltpu.make_async_remote_copy(
            src_ref=sums.at[turn, me],
            dst_ref=sums.at[turn, source],
            send_sem=send_sem.at[2 * turn + 1, k - 1],
            recv_sem=recv_sem.at[2 * turn + 1, k - 1],
            device_id=place(partner(k)),
            device_id_type=pl.DeviceIdType.MESH,
        )

    def start_scatter(turn, image):
        for owner in range(n):
            column, block = owner // per_column, owner % per_column
            stage[turn, owner] = image[block * rows : (block + 1) * rows, column * LANES : (column + 1) * LANES]
        for k in odds:
            scatter_copy(turn, k).start()
        for k in odds:
            scatter_copy(turn, k).wait_recv()
            stage[turn, partner(k - 1)] = stage[turn, partner(k - 1)] + pairs[turn, k // 2]
            if k > 1:
                scatter_copy(turn, k - 1).start()

    def start_gather(turn):
        for k in odds[:-1]:
            scatter_copy(turn, k - 1).wait_recv()
        terms = [stage[turn, me]] + [parts[turn, k] for k in range(n // 2 - 1)]
        while len(terms) > 1:
            terms = [a + b for a, b in zip(terms[::2], terms[1::2])] + ([terms[-1]] if len(terms) % 2 else [])
        sums[turn, me] = terms[0]
        for k in direct:
            gather_copy(turn, k).start()
        for k in order:
            scatter_copy(turn, k).wait_send()

    def gathered(turn):
        for k in direct:
            gather_arrival(turn, k).wait_recv()
            if k > 1:
                relay_copy(turn, k).start()
        for k in direct:
            if k > 1:
                relay_copy(turn, k).wait_recv()
        blocks = [sums[turn, owner] for owner in range(n)]
        columns = [jnp.concatenate(blocks[at : at + per_column], axis=0) for at in range(0, n, per_column)]
        return jnp.concatenate(columns, axis=1)

    start_scatter(0, image_of(start_ref[...]))
    start_gather(0)
    image = gathered(0)
    start_scatter(1, image_of(image))
    start_gather(1)
    inverse = inverse_cholesky(mm_nt(image, image))
    image = mm(inverse, gathered(1))
    basis = mm(inverse_cholesky(mm_nt(image, image)), image)
    factor_ref[...] = basis

    truncated = None
    for part in range(n_gx):
        term = mm_nt(held(part), basis[:, part * width : (part + 1) * width])
        truncated = term if truncated is None else truncated + term
    share = cells_z // n
    for s in range(species):
        for line in range(lines):
            at = (s * lines + line) * cells_z
            core_out[:, line, s * rank : (s + 1) * rank] = truncated[at : at + cells_z]

    mine = my_yz * n_gx + my_x

    def core_copy(k):
        peer = partner(k)
        return pltpu.make_async_remote_copy(
            src_ref=core_out.at[pl.ds(peer * share, share)],
            dst_ref=core_in.at[mine],
            send_sem=send_sem.at[4, k - 1],
            recv_sem=recv_sem.at[4, k - 1],
            device_id=place(peer),
            device_id_type=pl.DeviceIdType.MESH,
        )

    def core_arrival(k):
        source = partner(k)
        place_of = lax.rem(source, n_yz) * n_gx + lax.div(source, n_yz)
        return pltpu.make_async_remote_copy(
            src_ref=core_out.at[pl.ds(partner(k) * share, share)],
            dst_ref=core_in.at[place_of],
            send_sem=send_sem.at[4, k - 1],
            recv_sem=recv_sem.at[4, k - 1],
            device_id=place(partner(k)),
            device_id_type=pl.DeviceIdType.MESH,
        )

    for k in order:
        core_copy(k).start()

    core_in[mine] = core_out[pl.ds(me * share, share)]

    for k in order:
        for turn in range(2):
            if k in direct:
                gather_copy(turn, k).wait_send()
            else:
                relay_copy(turn, k - 1).wait_send()
        core_arrival(k).wait()

    core_ref[...] = core_in[...]


def kernel_program(tensor, start_basis, n_gx, n_yz, rows):
    n = n_gx * n_yz
    species, width, lines_held, cells_z = tensor.shape
    rank, total = start_basis.shape
    lines = lines_held // n_gx
    cell_count = species * lines_held * n_yz * cells_z
    share = cells_z // n
    out = species * rank
    core, factor = pl.pallas_call(
        functools.partial(kernel, (n_gx, n_yz, cell_count, rows)),
        out_shape=(
            pltpu.VMEM((n, share, lines, out), jnp.float32),
            pltpu.VMEM((rank, total), jnp.float32),
        ),
        in_specs=[pl.BlockSpec(memory_space=pltpu.VMEM)] * 2,
        out_specs=(pl.BlockSpec(memory_space=pltpu.VMEM),) * 2,
        scratch_shapes=[
            pltpu.VMEM((n_gx, species, lines, cells_z, width), jnp.float32),
            pltpu.VMEM((2, n, rows, LANES), jnp.float32),
            pltpu.VMEM((2, n, rows, LANES), jnp.float32),
            pltpu.VMEM((2, n // 2, rows, LANES), jnp.float32),
            pltpu.VMEM((2, n // 2 - 1, rows, LANES), jnp.float32),
            pltpu.VMEM((cells_z, lines, out), jnp.float32),
            pltpu.VMEM((n, share, lines, out), jnp.float32),
            pltpu.SemaphoreType.DMA((n_gx - 1,)),
            pltpu.SemaphoreType.DMA((n_gx - 1,)),
            pltpu.SemaphoreType.DMA((5, n - 1)),
            pltpu.SemaphoreType.DMA((5, n - 1)),
        ],
        compiler_params=pltpu.CompilerParams(collective_id=0, has_side_effects=True),
    )(tensor.transpose(0, 2, 3, 1), start_basis)
    core = core.transpose(1, 0, 2, 3).reshape(share, n * lines, out)
    return core, factor


def orthonormal(image_rows):
    small_gram = jnp.dot(image_rows, image_rows.T, precision=HIGHEST)
    lower_factor = jnp.linalg.cholesky(small_gram)
    return lax.linalg.triangular_solve(lower_factor, image_rows, left_side=True, lower=True)


def collective_program(tensor, start_basis):
    regrouped = lax.all_to_all(tensor, "gx", split_axis=2, concat_axis=1, tiled=True)
    species, _, lines, cells_z = regrouped.shape
    cell_count = species * lines * lax.axis_size("gx") * lax.axis_size("yz") * cells_z
    gram_matrix = lax.dot_general(
        regrouped, regrouped, (((0, 2, 3), (0, 2, 3)), ((), ())), precision=HIGHEST
    )
    gram_matrix = lax.psum(gram_matrix, ("gx", "yz")) / cell_count
    basis = start_basis
    for _ in range(2):
        basis = orthonormal(jnp.dot(basis, gram_matrix, precision=HIGHEST))
    core_local = jnp.einsum("kx,sxyz->zysk", basis, regrouped, precision=HIGHEST)
    core_local = core_local.reshape(cells_z, lines, species * basis.shape[0])
    core_tensor = lax.all_to_all(
        lax.all_to_all(core_local, "gx", split_axis=0, concat_axis=1, tiled=True),
        "yz",
        split_axis=0,
        concat_axis=1,
        tiled=True,
    )
    return core_tensor, basis


def solution(mesh):
    n_gx, n_yz = mesh.shape["gx"], mesh.shape["yz"]
    n = n_gx * n_yz

    def local(tensor, start_basis):
        rank, total = start_basis.shape
        rows, left_over = divmod(rank * (total // LANES), n)
        whole_rows = left_over == 0 and total % LANES == 0 and n & (n - 1) == 0
        whole_rows = whole_rows and rank % max(rows, 1) == 0 and rank % SUBLANES == 0
        if whole_rows and tensor.shape[1] % LANES == 0:
            return kernel_program(tensor, start_basis, n_gx, n_yz, rows)
        return collective_program(tensor, start_basis)

    return jax.shard_map(
        local,
        mesh=mesh,
        in_specs=(P(None, "gx", "yz", None), P()),
        out_specs=(P(("gx", "yz"), None, None), P()),
        check_vma=False,
    )
```
